32 devices in a mesh: dp: 4 (over y, x), seq: 2 (over core), stream: 4 (over z).
Axes of the slice: x: 2, y: 2, z: 4, core: 2. Of those that a mesh axis runs over, the one named last changes fastest.
Arguments:
- tokens: bfloat16 [4096, 6144], P(('dp', 'seq', 'stream')), parts along dimension 0, may hold values from -800 to 800
- norm_gain: float32 [6144], replicated, may hold values from 0.25 to 1.75
- qkv_weight: bfloat16 [3, 6144, 3072], P(None, None, 'stream'), may hold values from -0.08930431 to 0.08930431
- query_gain: float32 [24, 128], P('stream'), may hold values from 0.4 to 6, as said below
- key_gain: float32 [24, 128], P('stream'), may hold values from 0.4 to 6, as said below
- out_weight: bfloat16 [3072, 6144], P('stream'), may hold values from -0.4375 to 0.4375
Outputs:
- attn_branch: bfloat16 [4096, 6144], P(('dp', 'seq', 'stream')), parts along dimension 0
The draws below stay inside these ranges and needn't reach their ends.
There are 4 independent parts, one for each index of `dp`. The reference program is written for one: setup_inputs(seed, part) draws one part's arguments, and reference() takes and returns one part's arrays. A program takes and returns all parts, laid end to end along the dimension named above; an argument that names none is the same for every part. Nothing has to cross between parts.
Inputs may be any that keep to these rules, and one draw needn't show every extreme that they name: `query_gain`: positive. `key_gain`: positive.
All inputs are finite; a program needn't handle non-finite values.
Results may differ from the reference program's by a relative error of at most 0.014.
Values may be sent and summed in bfloat16 or wider, within the bound.
A program may use at most 192 MiB of HBM per device.

```python
import jax
import jax.numpy as jnp
from jax import lax

D = 6144
HS = 128
HEADS = 24
LENGTH = 1024


def draw_gain_common(key, salt):
    lowest = jnp.log(jnp.float32(1.0))
    highest = jnp.log(jnp.float32(2.0))
    return jnp.exp(jax.random.uniform(jax.random.fold_in(key, salt), (HEADS, HS), jnp.float32, lowest, highest))


def draw_query_gain(key, part):
    return draw_gain_common(key, 1)


def draw_key_gain(key, part):
    return draw_gain_common(key, 2)


def draw_qkv_weight(key, part):
    base = jnp.clip(jax.random.normal(jax.random.fold_in(key, 3), (3, D, HEADS * HS), jnp.float32), -6.0, 6.0)
    base = base * float(D) ** (-0.5)
    return base.astype(jnp.bfloat16)


def draw_tokens(key, part):
    normal_part = jnp.clip(jax.random.normal(jax.random.fold_in(key, 4), (LENGTH, D), jnp.float32), -6.0, 6.0)
    return normal_part.astype(jnp.bfloat16)


def shard_levels(key, shape, split, low, top_value):
    def one(position, parts):
        draws = jax.random.uniform(jax.random.fold_in(jax.random.fold_in(key, 6), position), (parts,), jnp.float32, low / len(split), top_value / len(split))
        return jnp.repeat(jnp.exp(draws), shape[position] // parts).reshape((-1,) + (1,) * (len(shape) - position - 1))

    factor_of = one(*split[0])
    for cut in split[1:]:
        factor_of = factor_of * one(*cut)
    return factor_of


def normal_values(own_key, shape, scale, reach, shards=(), dtype=jnp.bfloat16):
    values = scale * jax.random.normal(own_key, shape, jnp.float32)
    if shards:
        values = values * shard_levels(own_key, shape, shards, -0.22, 0.18)
    return jnp.clip(values, -reach, reach).astype(dtype)


def setup_inputs(seed: int = 0, part: int = 0) -> dict:
    streams_of = jax.random.split(jax.random.key(seed), 7)
    own_keys = jax.random.split(jax.random.fold_in(streams_of[6], part), 7)
    tokens = draw_tokens(jax.random.fold_in(jax.random.fold_in(streams_of[6], part), 71), part)
    norm_gain = jnp.clip(1.0 + 0.15 * jax.random.normal(streams_of[1], (D,), jnp.float32), 0.25, 1.75)
    qkv_weight = draw_qkv_weight(jax.random.fold_in(streams_of[6], 71), part)
    query_gain = draw_query_gain(jax.random.fold_in(streams_of[6], 71), part)
    key_gain = draw_key_gain(jax.random.fold_in(streams_of[6], 71), part)
    out_weight = normal_values(streams_of[5], (HEADS * HS, D), (HEADS * HS // 16) ** -0.5, 0.4375, ((0, 4),))
    return {"tokens": tokens, "norm_gain": norm_gain, "qkv_weight": qkv_weight, "query_gain": query_gain, "key_gain": key_gain, "out_weight": out_weight}


def head_layer_norm(raw_proj, gain):
    shaped = raw_proj.reshape(raw_proj.shape[0], HEADS, HS)
    head_mean = lax.optimization_barrier(jnp.mean(shaped, axis=-1, keepdims=True))
    centred = shaped - head_mean
    head_var = lax.optimization_barrier(jnp.mean(centred * centred, axis=-1, keepdims=True))
    return (centred * lax.rsqrt(head_var + 1e-06) * gain[None, :, :]).astype(jnp.bfloat16)

def one_head(operands):
    queries, keys_all, values_all = operands
    scores = jnp.dot(queries, keys_all.T, preferred_element_type=jnp.float32) * (1.0 / math_sqrt(HS))
    row_peak = lax.optimization_barrier(jnp.max(scores, axis=-1, keepdims=True))
    probs = jnp.exp(scores - row_peak)
    numer = jnp.dot(probs.astype(jnp.bfloat16), values_all, preferred_element_type=jnp.float32)
    return (numer / lax.optimization_barrier(jnp.sum(probs, axis=-1, keepdims=True))).astype(jnp.bfloat16)

def math_sqrt(value):
    return float(value) ** 0.5

def reference(tokens, norm_gain, qkv_weight, query_gain, key_gain, out_weight):
    inputs = tokens.astype(jnp.float32)
    row_mean = lax.optimization_barrier(jnp.mean(inputs, axis=-1, keepdims=True))
    centred = inputs - row_mean
    row_var = lax.optimization_barrier(jnp.mean(centred * centred, axis=-1, keepdims=True))
    normed = (centred * lax.rsqrt(row_var + 1e-06) * norm_gain[None, :]).astype(jnp.bfloat16)
    raw_query = jnp.dot(normed, qkv_weight[0], preferred_element_type=jnp.float32)
    raw_key = jnp.dot(normed, qkv_weight[1], preferred_element_type=jnp.float32)
    raw_value = jnp.dot(normed, qkv_weight[2], preferred_element_type=jnp.float32)
    queries = head_layer_norm(raw_query, query_gain)
    keys_all = head_layer_norm(raw_key, key_gain)
    values_all = raw_value.astype(jnp.bfloat16).reshape(LENGTH, HEADS, HS)
    stacked = (jnp.transpose(queries, (1, 0, 2)), jnp.transpose(keys_all, (1, 0, 2)), jnp.transpose(values_all, (1, 0, 2)))
    per_head = lax.map(one_head, stacked)
    attended = jnp.transpose(per_head, (1, 0, 2)).reshape(LENGTH, HEADS * HS)
    return jnp.dot(attended, out_weight, preferred_element_type=jnp.float32).astype(jnp.bfloat16)
```

```python
import jax
import jax.numpy as jnp
from jax import lax
from jax.sharding import PartitionSpec as P


def head_layer_norm(raw_proj, gain):
    local_heads = gain.shape[0]
    head_size = gain.shape[1]
    shaped = raw_proj.reshape(raw_proj.shape[0], local_heads, head_size)
    head_mean = jnp.mean(shaped, axis=-1, keepdims=True)
    centred = shaped - head_mean
    head_var = jnp.mean(centred * centred, axis=-1, keepdims=True)
    return (centred * lax.rsqrt(head_var + 1e-06) * gain[None, :, :]).astype(jnp.bfloat16)


def attend(queries, keys, values, scaling):
    scores = (
        jnp.einsum("qhd,khd->qhk", queries, keys, preferred_element_type=jnp.float32) * scaling
    )
    peak = jnp.max(scores, axis=-1, keepdims=True)
    probs = jnp.exp(scores - peak)
    total = jnp.sum(probs, axis=-1)
    weighted = jnp.einsum(
        "qhk,khd->qhd", probs.astype(jnp.bfloat16), values, preferred_element_type=jnp.float32
    )
    return (weighted / total[..., None]).astype(jnp.bfloat16)


def on_device(tokens, norm_gain, qkv_weight, query_gain, key_gain, out_weight):
    inputs = tokens.astype(jnp.float32)
    row_mean = jnp.mean(inputs, axis=-1, keepdims=True)
    centred = inputs - row_mean
    row_var = jnp.mean(centred * centred, axis=-1, keepdims=True)
    normed = (centred * lax.rsqrt(row_var + 1e-06) * norm_gain[None, :]).astype(jnp.bfloat16)
    local_heads, head_size = query_gain.shape
    rows = tokens.shape[0]
    width = local_heads * head_size
    count = lax.axis_size("stream")
    place = lax.axis_index("stream")
    cores = lax.axis_size("seq")
    scaling = 1.0 / float(head_size) ** 0.5

    def rightward(value, first, last):
        return lax.ppermute(value, "stream", [(i, i + 1) for i in range(first, last)])

    def leftward(value, first, last):
        return lax.ppermute(value, "stream", [(i, i - 1) for i in range(first, last, -1)])

    from_left, from_right = [normed], [normed]
    for step in range(1, count):
        from_left.append(rightward(from_left[-1], step - 1, count - 1))
        from_right.append(leftward(from_right[-1], count - step, 0))

    def either(step):
        return jnp.where(place >= step, from_left[step], from_right[step])

    half = count // 2
    longest = jnp.maximum(place, count - 1 - place)
    slots = [(normed, place)]
    for step in range(1, half + 1):
        if step < count:
            slots.append((either(step), jnp.where(place >= step, place - step, place + step)))
    for extra in range(1, count - half):
        step, other = half + extra, half - extra
        far = longest >= step
        slots.append(
            (
                jnp.where(far, either(step), from_right[other]),
                jnp.where(
                    far,
                    jnp.where(place >= step, place - step, place + step),
                    place + other,
                ),
            )
        )

    queries = jnp.zeros((count * rows, local_heads, head_size), jnp.bfloat16)
    keys, values = [], []
    for shard, origin in slots:
        raw = jnp.einsum("nd,cdk->cnk", shard, qkv_weight, preferred_element_type=jnp.float32)
        queries = lax.dynamic_update_slice_in_dim(
            queries, head_layer_norm(raw[0], query_gain), origin * rows, 0
        )
        key_now = head_layer_norm(raw[1], key_gain)
        value_now = raw[2].astype(jnp.bfloat16)
        both = jnp.concatenate([key_now.reshape(rows, width), value_now], axis=1)
        held = [both]
        for turn in range(1, cores):
            held.append(lax.ppermute(both, "seq", [(i, (i + turn) % cores) for i in range(cores)]))
        for piece in held:
            keys.append(piece[:, :width])
            values.append(piece[:, width:])
    keys_all = jnp.concatenate(keys, 0).reshape(-1, local_heads, head_size)
    values_all = jnp.concatenate(values, 0).reshape(-1, local_heads, head_size)

    attended = attend(queries, keys_all, values_all, scaling).reshape(count * rows, width)

    def share(block):
        piece = lax.dynamic_slice_in_dim(attended, block * rows, rows, 0)
        return jnp.dot(piece, out_weight, preferred_element_type=jnp.float32)

    got_left = got_right = None
    for step in range(1, count):
        right_sum = share(lax.rem(place - step + count, count))
        left_sum = share(lax.rem(place + step, count))
        if got_left is not None:
            right_sum = right_sum + got_left
            left_sum = left_sum + got_right
        right_sum, left_sum = lax.optimization_barrier(
            (right_sum.astype(jnp.bfloat16), left_sum.astype(jnp.bfloat16))
        )
        got_left = rightward(right_sum, 0, step)
        got_right = leftward(left_sum, count - 1, count - 1 - step)
    result = share(place)
    if got_left is not None:
        result = result + got_left + got_right
    return result.astype(jnp.bfloat16)


def solution(mesh):
    placed = (
        P(("dp", "seq", "stream"), None),
        P(),
        P(None, None, "stream"),
        P("stream", None),
        P("stream", None),
        P("stream", None),
    )

    return jax.shard_map(
        on_device,
        mesh=mesh,
        in_specs=placed,
        out_specs=P(("dp", "seq", "stream"), None),
        check_vma=False,
    )
```

```python
import functools

import jax
import jax.numpy as jnp
from jax import lax
from jax.experimental import pallas as pl
from jax.experimental.pallas import tpu as pltpu
from jax.sharding import PartitionSpec as P


def project_kernel(head_size, x_ref, w_ref, qg_ref, kg_ref, q_ref, kv_ref):
    shard = x_ref[...]
    raw = [jnp.dot(shard, w_ref[c], preferred_element_type=jnp.float32) for c in range(3)]

    def normal(part, gain):
        centred = part - jnp.mean(part, axis=-1, keepdims=True)
        var = jnp.mean(centred * centred, axis=-1, keepdims=True)
        return (centred * lax.rsqrt(var + 1e-06) * gain).astype(jnp.bfloat16)

    for start in range(0, q_ref.shape[1], head_size):
        cols = slice(start, start + head_size)
        q_ref[:, cols] = normal(raw[0][:, cols], qg_ref[:, cols])
        kv_ref[0, :, cols] = normal(raw[1][:, cols], kg_ref[:, cols])
    kv_ref[1] = raw[2].astype(jnp.bfloat16)


def project(shard, weight, query_gain, key_gain, head_size):
    rows, depth = shard.shape
    width = weight.shape[2]
    block = 2 * head_size if width % (2 * head_size) == 0 else head_size
    return pl.pallas_call(
        functools.partial(project_kernel, head_size),
        grid=(width // block,),
        in_specs=[
            pl.BlockSpec((rows, depth), lambda g: (0, 0)),
            pl.BlockSpec((3, depth, block), lambda g: (0, 0, g)),
            pl.BlockSpec((1, block), lambda g: (0, g)),
            pl.BlockSpec((1, block), lambda g: (0, g)),
        ],
        out_specs=[
            pl.BlockSpec((rows, block), lambda g: (0, g)),
            pl.BlockSpec((2, rows, block), lambda g: (0, 0, g)),
        ],
        out_shape=[
            jax.ShapeDtypeStruct((rows, width), jnp.bfloat16),
            jax.ShapeDtypeStruct((2, rows, width), jnp.bfloat16),
        ],
        compiler_params=pltpu.CompilerParams(vmem_limit_bytes=40 << 20),
        cost_estimate=pl.CostEstimate(
            flops=6 * rows * depth * width, bytes_accessed=6 * depth * width, transcendentals=0
        ),
        name="project",
    )(shard, weight, query_gain, key_gain)


def attend_kernel(n_queries, scaling, *refs):
    query_refs, kv_refs, out_ref = refs[:n_queries], refs[n_queries:-1], refs[-1]
    keys = jnp.concatenate([ref[0] for ref in kv_refs], axis=0)
    values = jnp.concatenate([ref[1] for ref in kv_refs], axis=0)
    rows = query_refs[0].shape[0]
    for number, ref in enumerate(query_refs):
        scores = (
            lax.dot_general(
                ref[...], keys, (((1,), (1,)), ((), ())), preferred_element_type=jnp.float32
            )
            * scaling
        )
        probs = jnp.exp(scores - jnp.max(scores, axis=-1, keepdims=True))
        total = jnp.sum(probs, axis=-1, keepdims=True)
        mixed = jnp.dot(probs.astype(jnp.bfloat16), values, preferred_element_type=jnp.float32)
        out_ref[number * rows : (number + 1) * rows, :] = (mixed / total).astype(jnp.bfloat16)


def attend(queries, pieces, head_size, scaling):
    rows, width = queries[0].shape
    total = rows * len(queries)
    keys = rows * len(pieces)
    return pl.pallas_call(
        functools.partial(attend_kernel, len(queries), scaling),
        grid=(width // head_size,),
        in_specs=[pl.BlockSpec((rows, head_size), lambda h: (0, h))] * len(queries)
        + [pl.BlockSpec((2, rows, head_size), lambda h: (0, 0, h))] * len(pieces),
        out_specs=pl.BlockSpec((total, head_size), lambda h: (0, h)),
        out_shape=jax.ShapeDtypeStruct((total, width), jnp.bfloat16),
        compiler_params=pltpu.CompilerParams(vmem_limit_bytes=40 << 20),
        cost_estimate=pl.CostEstimate(
            flops=4 * total * keys * width,
            bytes_accessed=4 * (total + keys) * width,
            transcendentals=total * keys * width // head_size,
        ),
        name="attend",
    )(*queries, *pieces)


def on_device(tokens, norm_gain, qkv_weight, query_gain, key_gain, out_weight):
    inputs = tokens.astype(jnp.float32)
    row_mean = jnp.mean(inputs, axis=-1, keepdims=True)
    centred = inputs - row_mean
    row_var = jnp.mean(centred * centred, axis=-1, keepdims=True)
    normed = (centred * lax.rsqrt(row_var + 1e-06) * norm_gain[None, :]).astype(jnp.bfloat16)
    local_heads, head_size = query_gain.shape
    rows = tokens.shape[0]
    width = local_heads * head_size
    count = lax.axis_size("stream")
    place = lax.axis_index("stream")
    cores = lax.axis_size("seq")
    scaling = 1.0 / float(head_size) ** 0.5

    def rightward(value, first, last):
        return lax.ppermute(value, "stream", [(i, i + 1) for i in range(first, last)])

    def leftward(value, first, last):
        return lax.ppermute(value, "stream", [(i, i - 1) for i in range(first, last, -1)])

    from_left, from_right = [normed], [normed]
    for step in range(1, count):
        from_left.append(rightward(from_left[-1], step - 1, count - 1))
        from_right.append(leftward(from_right[-1], count - step, 0))

    def either(step):
        return jnp.where(place >= step, from_left[step], from_right[step])

    half = count // 2
    longest = jnp.maximum(place, count - 1 - place)
    slots = [(normed, place)]
    for step in range(1, half + 1):
        if step < count:
            shard, from_right[step] = lax.optimization_barrier((either(step), from_right[step]))
            slots.append((shard, jnp.where(place >= step, place - step, place + step)))
    for extra in range(1, count - half):
        step, other = half + extra, half - extra
        far = longest >= step
        slots.append(
            (
                jnp.where(far, either(step), from_right[other]),
                jnp.where(
                    far,
                    jnp.where(place >= step, place - step, place + step),
                    place + other,
                ),
            )
        )

    gains = query_gain.reshape(1, width), key_gain.reshape(1, width)
    queries, pieces = [], []
    for shard, origin in slots:
        query_now, both = project(shard, qkv_weight, *gains, head_size)
        queries.append(query_now)
        pieces.append(both)
        for turn in range(1, cores):
            pieces.append(
                lax.ppermute(both, "seq", [(i, (i + turn) % cores) for i in range(cores)])
            )
    attended = attend(queries, pieces, head_size, scaling)

    def share(block):
        slot = sum(number * (origin == block) for number, (_, origin) in enumerate(slots))
        piece = lax.dynamic_slice_in_dim(attended, slot * rows, rows, 0)
        return lax.optimization_barrier(
            jnp.dot(piece, out_weight, preferred_element_type=jnp.float32)
        )

    got_left = got_right = None
    for step in range(1, count):
        right_sum = share(lax.rem(place - step + count, count))
        left_sum = share(lax.rem(place + step, count))
        if got_left is not None:
            right_sum = right_sum + got_left
            left_sum = left_sum + got_right
        right_sum, left_sum = lax.optimization_barrier(
            (right_sum.astype(jnp.bfloat16), left_sum.astype(jnp.bfloat16))
        )
        got_left = rightward(right_sum, 0, step)
        got_right = leftward(left_sum, count - 1, count - 1 - step)
    result = share(place)
    if got_left is not None:
        result = result + got_left + got_right
    return result.astype(jnp.bfloat16)


def solution(mesh):
    placed = (
        P(("dp", "seq", "stream"), None),
        P(),
        P(None, None, "stream"),
        P("stream", None),
        P("stream", None),
        P("stream", None),
    )

    return jax.shard_map(
        on_device,
        mesh=mesh,
        in_specs=placed,
        out_specs=P(("dp", "seq", "stream"), None),
        check_vma=False,
    )
```

```python
import functools

import jax
import jax.numpy as jnp
from jax import lax
from jax.experimental import pallas as pl
from jax.experimental.pallas import tpu as pltpu
from jax.sharding import PartitionSpec as P


def project_kernel(head_size, x_ref, w_ref, qg_ref, kg_ref, q_ref, kv_ref):
    shard = x_ref[...]
    raw = [jnp.dot(shard, w_ref[c], preferred_element_type=jnp.float32) for c in range(3)]

    def normal(part, gain):
        centred = part - jnp.mean(part, axis=-1, keepdims=True)
        var = jnp.mean(centred * centred, axis=-1, keepdims=True)
        return (centred * lax.rsqrt(var + 1e-06) * gain).astype(jnp.bfloat16)

    for start in range(0, q_ref.shape[1], head_size):
        cols = slice(start, start + head_size)
        q_ref[:, cols] = normal(raw[0][:, cols], qg_ref[:, cols])
        kv_ref[0, :, cols] = normal(raw[1][:, cols], kg_ref[:, cols])
    kv_ref[1] = raw[2].astype(jnp.bfloat16)


def project(shard, weight, query_gain, key_gain, head_size):
    rows, depth = shard.shape
    width = weight.shape[2]
    block = 2 * head_size if width % (2 * head_size) == 0 else head_size
    return pl.pallas_call(
        functools.partial(project_kernel, head_size),
        grid=(width // block,),
        in_specs=[
            pl.BlockSpec((rows, depth), lambda g: (0, 0)),
            pl.BlockSpec((3, depth, block), lambda g: (0, 0, g)),
            pl.BlockSpec((1, block), lambda g: (0, g)),
            pl.BlockSpec((1, block), lambda g: (0, g)),
        ],
        out_specs=[
            pl.BlockSpec((rows, block), lambda g: (0, g)),
            pl.BlockSpec((2, rows, block), lambda g: (0, 0, g)),
        ],
        out_shape=[
            jax.ShapeDtypeStruct((rows, width), jnp.bfloat16),
            jax.ShapeDtypeStruct((2, rows, width), jnp.bfloat16),
        ],
        compiler_params=pltpu.CompilerParams(vmem_limit_bytes=40 << 20),
        cost_estimate=pl.CostEstimate(
            flops=6 * rows * depth * width, bytes_accessed=6 * depth * width, transcendentals=0
        ),
        name="project",
    )(shard, weight, query_gain, key_gain)


def attend_kernel(n_queries, scaling, *refs):
    query_refs, kv_refs, out_ref = refs[:n_queries], refs[n_queries:-1], refs[-1]
    keys = jnp.concatenate([ref[0] for ref in kv_refs], axis=0)
    values = jnp.concatenate([ref[1] for ref in kv_refs], axis=0)
    rows = query_refs[0].shape[0]
    for number, ref in enumerate(query_refs):
        scores = (
            lax.dot_general(
                ref[...], keys, (((1,), (1,)), ((), ())), preferred_element_type=jnp.float32
            )
            * scaling
        )
        probs = jnp.exp(scores - jnp.max(scores, axis=-1, keepdims=True))
        total = jnp.sum(probs, axis=-1, keepdims=True)
        mixed = jnp.dot(probs.astype(jnp.bfloat16), values, preferred_element_type=jnp.float32)
        out_ref[number * rows : (number + 1) * rows, :] = (mixed / total).astype(jnp.bfloat16)


def attend(queries, pieces, head_size, scaling):
    rows, width = queries[0].shape
    total = rows * len(queries)
    keys = rows * len(pieces)
    return pl.pallas_call(
        functools.partial(attend_kernel, len(queries), scaling),
        grid=(width // head_size,),
        in_specs=[pl.BlockSpec((rows, head_size), lambda h: (0, h))] * len(queries)
        + [pl.BlockSpec((2, rows, head_size), lambda h: (0, 0, h))] * len(pieces),
        out_specs=pl.BlockSpec((total, head_size), lambda h: (0, h)),
        out_shape=jax.ShapeDtypeStruct((total, width), jnp.bfloat16),
        compiler_params=pltpu.CompilerParams(vmem_limit_bytes=60 << 20),
        cost_estimate=pl.CostEstimate(
            flops=4 * total * keys * width,
            bytes_accessed=4 * (total + keys) * width,
            transcendentals=total * keys * width // head_size,
        ),
        name="attend",
    )(*queries, *pieces)


def on_device(tokens, norm_gain, qkv_weight, query_gain, key_gain, out_weight):
    inputs = tokens.astype(jnp.float32)
    row_mean = jnp.mean(inputs, axis=-1, keepdims=True)
    centred = inputs - row_mean
    row_var = jnp.mean(centred * centred, axis=-1, keepdims=True)
    normed = (centred * lax.rsqrt(row_var + 1e-06) * norm_gain[None, :]).astype(jnp.bfloat16)
    local_heads, head_size = query_gain.shape
    rows = tokens.shape[0]
    width = local_heads * head_size
    count = lax.axis_size("stream")
    place = lax.axis_index("stream")
    cores = lax.axis_size("seq")
    scaling = 1.0 / float(head_size) ** 0.5

    def rightward(value, first, last):
        return lax.ppermute(value, "stream", [(i, i + 1) for i in range(first, last)])

    def leftward(value, first, last):
        return lax.ppermute(value, "stream", [(i, i - 1) for i in range(first, last, -1)])

    from_left, from_right = [normed], [normed]
    for step in range(1, count):
        from_left.append(rightward(from_left[-1], step - 1, count - 1))
        from_right.append(leftward(from_right[-1], count - step, 0))

    def either(step):
        return jnp.where(place >= step, from_left[step], from_right[step])

    half = count // 2
    longest = jnp.maximum(place, count - 1 - place)
    slots = [(normed, place)]
    for step in range(1, half + 1):
        if step < count:
            shard, from_right[step] = lax.optimization_barrier((either(step), from_right[step]))
            slots.append((shard, jnp.where(place >= step, place - step, place + step)))
    for extra in range(1, count - half):
        step, other = half + extra, half - extra
        far = longest >= step
        slots.append(
            (
                jnp.where(far, either(step), from_right[other]),
                jnp.where(
                    far,
                    jnp.where(place >= step, place - step, place + step),
                    place + other,
                ),
            )
        )

    gains = query_gain.reshape(1, width), key_gain.reshape(1, width)
    queries, pieces = [], []
    for shard, origin in slots:
        query_now, both = project(shard, qkv_weight, *gains, head_size)
        queries.append(query_now)
        pieces.append(both)
        for turn in range(1, cores):
            pieces.append(
                lax.ppermute(both, "seq", [(i, (i + turn) % cores) for i in range(cores)])
            )
    attended = attend(queries, pieces, head_size, scaling)

    def share(block):
        slot = sum(number * (origin == block) for number, (_, origin) in enumerate(slots))
        piece = lax.dynamic_slice_in_dim(attended, slot * rows, rows, 0)
        return jnp.dot(piece, out_weight, preferred_element_type=jnp.float32)

    got_left = got_right = None
    for step in range(1, count):
        right_block = lax.rem(place - step + count, count)
        left_block = lax.rem(place + step, count)
        if 2 * step <= count:
            block = jnp.where(place < step, right_block, left_block)
            right_sum = share(block)
            if got_left is not None:
                right_sum = lax.optimization_barrier(right_sum) + got_left + got_right
            left_sum = right_sum = right_sum.astype(jnp.bfloat16)
        else:
            right_sum = lax.optimization_barrier(share(right_block))
            left_sum = lax.optimization_barrier(share(left_block))
            if got_left is not None:
                right_sum, left_sum = right_sum + got_left, left_sum + got_right
            right_sum, left_sum = lax.optimization_barrier(
                (right_sum.astype(jnp.bfloat16), left_sum.astype(jnp.bfloat16))
            )
        got_left = rightward(right_sum, 0, step)
        got_right = leftward(left_sum, count - 1, count - 1 - step)
    result = lax.optimization_barrier(share(place))
    if got_left is not None:
        result = result + got_left + got_right
    return result.astype(jnp.bfloat16)


def solution(mesh):
    placed = (
        P(("dp", "seq", "stream"), None),
        P(),
        P(None, None, "stream"),
        P("stream", None),
        P("stream", None),
        P("stream", None),
    )

    return jax.shard_map(
        on_device,
        mesh=mesh,
        in_specs=placed,
        out_specs=P(("dp", "seq", "stream"), None),
        check_vma=False,
    )
```

```python
import functools

import jax
import jax.numpy as jnp
from jax import lax
from jax.experimental import pallas as pl
from jax.experimental.pallas import tpu as pltpu
from jax.sharding import PartitionSpec as P


def project_kernel(head_size, x_ref, w_ref, qg_ref, kg_ref, q_ref, kv_ref):
    shard = x_ref[...]
    raw = [jnp.dot(shard, w_ref[c], preferred_element_type=jnp.float32) for c in range(3)]

    def normal(part, gain):
        centred = part - jnp.mean(part, axis=-1, keepdims=True)
        var = jnp.mean(centred * centred, axis=-1, keepdims=True)
        return (centred * lax.rsqrt(var + 1e-06) * gain).astype(jnp.bfloat16)

    for start in range(0, q_ref.shape[1], head_size):
        cols = slice(start, start + head_size)
        q_ref[:, cols] = normal(raw[0][:, cols], qg_ref[:, cols])
        kv_ref[0, :, cols] = normal(raw[1][:, cols], kg_ref[:, cols])
    kv_ref[1] = raw[2].astype(jnp.bfloat16)


def project(shard, weight, query_gain, key_gain, head_size):
    rows, depth = shard.shape
    width = weight.shape[2]
    block = 2 * head_size if width % (2 * head_size) == 0 else head_size
    return pl.pallas_call(
        functools.partial(project_kernel, head_size),
        grid=(width // block,),
        in_specs=[
            pl.BlockSpec((rows, depth), lambda g: (0, 0)),
            pl.BlockSpec((3, depth, block), lambda g: (0, 0, g)),
            pl.BlockSpec((1, block), lambda g: (0, g)),
            pl.BlockSpec((1, block), lambda g: (0, g)),
        ],
        out_specs=[
            pl.BlockSpec((rows, block), lambda g: (0, g)),
            pl.BlockSpec((2, rows, block), lambda g: (0, 0, g)),
        ],
        out_shape=[
            jax.ShapeDtypeStruct((rows, width), jnp.bfloat16),
            jax.ShapeDtypeStruct((2, rows, width), jnp.bfloat16),
        ],
        compiler_params=pltpu.CompilerParams(vmem_limit_bytes=40 << 20),
        cost_estimate=pl.CostEstimate(
            flops=6 * rows * depth * width, bytes_accessed=6 * depth * width, transcendentals=0
        ),
        name="project",
    )(shard, weight, query_gain, key_gain)


def attend_kernel(n_queries, scaling, *refs):
    query_refs, kv_refs, out_ref = refs[:n_queries], refs[n_queries:-1], refs[-1]
    keys = jnp.concatenate([ref[0] for ref in kv_refs], axis=0)
    values = jnp.concatenate([ref[1] for ref in kv_refs], axis=0)
    pair = 2 if n_queries % 2 == 0 else 1
    rows = query_refs[0].shape[0] * pair
    for number in range(n_queries // pair):
        group = [ref[...] for ref in query_refs[number * pair : (number + 1) * pair]]
        scores = (
            lax.dot_general(
                jnp.concatenate(group, axis=0), keys, (((1,), (1,)), ((), ())), preferred_element_type=jnp.float32
            )
            * scaling
        )
        probs = jnp.exp(scores - jnp.max(scores, axis=-1, keepdims=True))
        total = jnp.sum(probs, axis=-1, keepdims=True)
        mixed = jnp.dot(probs.astype(jnp.bfloat16), values, preferred_element_type=jnp.float32)
        out_ref[number * rows : (number + 1) * rows, :] = (mixed / total).astype(jnp.bfloat16)


def attend(queries, pieces, head_size, scaling):
    rows, width = queries[0].shape
    total = rows * len(queries)
    keys = rows * len(pieces)
    return pl.pallas_call(
        functools.partial(attend_kernel, len(queries), scaling),
        grid=(width // head_size,),
        in_specs=[pl.BlockSpec((rows, head_size), lambda h: (0, h))] * len(queries)
        + [pl.BlockSpec((2, rows, head_size), lambda h: (0, 0, h))] * len(pieces),
        out_specs=pl.BlockSpec((total, head_size), lambda h: (0, h)),
        out_shape=jax.ShapeDtypeStruct((total, width), jnp.bfloat16),
        compiler_params=pltpu.CompilerParams(vmem_limit_bytes=60 << 20),
        cost_estimate=pl.CostEstimate(
            flops=4 * total * keys * width,
            bytes_accessed=4 * (total + keys) * width,
            transcendentals=total * keys * width // head_size,
        ),
        name="attend",
    )(*queries, *pieces)


def on_device(tokens, norm_gain, qkv_weight, query_gain, key_gain, out_weight):
    inputs = tokens.astype(jnp.float32)
    row_mean = jnp.mean(inputs, axis=-1, keepdims=True)
    centred = inputs - row_mean
    row_var = jnp.mean(centred * centred, axis=-1, keepdims=True)
    normed = (centred * lax.rsqrt(row_var + 1e-06) * norm_gain[None, :]).astype(jnp.bfloat16)
    local_heads, head_size = query_gain.shape
    rows = tokens.shape[0]
    width = local_heads * head_size
    count = lax.axis_size("stream")
    place = lax.axis_index("stream")
    cores = lax.axis_size("seq")
    scaling = 1.0 / float(head_size) ** 0.5

    def rightward(value, first, last):
        return lax.ppermute(value, "stream", [(i, i + 1) for i in range(first, last)])

    def leftward(value, first, last):
        return lax.ppermute(value, "stream", [(i, i - 1) for i in range(first, last, -1)])

    from_left, from_right = [normed], [normed]
    for step in range(1, count):
        from_left.append(rightward(from_left[-1], step - 1, count - 1))
        from_right.append(leftward(from_right[-1], count - step, 0))

    def either(step):
        return jnp.where(place >= step, from_left[step], from_right[step])

    half = count // 2
    longest = jnp.maximum(place, count - 1 - place)
    slots = [(normed, place)]
    for step in range(1, half + 1):
        if step < count:
            shard, from_right[step] = lax.optimization_barrier((either(step), from_right[step]))
            slots.append((shard, jnp.where(place >= step, place - step, place + step)))
    for extra in range(1, count - half):
        step, other = half + extra, half - extra
        far = longest >= step
        slots.append(
            (
                jnp.where(far, either(step), from_right[other]),
                jnp.where(
                    far,
                    jnp.where(place >= step, place - step, place + step),
                    place + other,
                ),
            )
        )

    gains = query_gain.reshape(1, width), key_gain.reshape(1, width)
    queries, pieces = [], []
    for shard, origin in slots:
        query_now, both = project(shard, qkv_weight, *gains, head_size)
        queries.append(query_now)
        pieces.append(both)
        for turn in range(1, cores):
            pieces.append(
                lax.ppermute(both, "seq", [(i, (i + turn) % cores) for i in range(cores)])
            )
    attended = attend(queries, pieces, head_size, scaling)

    def share(block):
        slot = sum(number * (origin == block) for number, (_, origin) in enumerate(slots))
        piece = lax.dynamic_slice_in_dim(attended, slot * rows, rows, 0)
        return jnp.dot(piece, out_weight, preferred_element_type=jnp.float32)

    got_left = got_right = None
    for step in range(1, count):
        right_block = lax.rem(place - step + count, count)
        left_block = lax.rem(place + step, count)
        if 2 * step <= count:
            block = jnp.where(place < step, right_block, left_block)
            right_sum = share(block)
            if got_left is not None:
                right_sum = lax.optimization_barrier(right_sum) + got_left + got_right
            left_sum = right_sum = right_sum.astype(jnp.bfloat16)
        else:
            right_sum = lax.optimization_barrier(share(right_block))
            left_sum = lax.optimization_barrier(share(left_block))
            if got_left is not None:
                right_sum, left_sum = right_sum + got_left, left_sum + got_right
            right_sum, left_sum = lax.optimization_barrier(
                (right_sum.astype(jnp.bfloat16), left_sum.astype(jnp.bfloat16))
            )
        got_left = rightward(right_sum, 0, step)
        got_right = leftward(left_sum, count - 1, count - 1 - step)
    result = lax.optimization_barrier(share(place))
    if got_left is not None:
        result = result + got_left + got_right
    return result.astype(jnp.bfloat16)


def solution(mesh):
    placed = (
        P(("dp", "seq", "stream"), None),
        P(),
        P(None, None, "stream"),
        P("stream", None),
        P("stream", None),
        P("stream", None),
    )

    return jax.shard_map(
        on_device,
        mesh=mesh,
        in_specs=placed,
        out_specs=P(("dp", "seq", "stream"), None),
        check_vma=False,
    )
```
